32 devices in a mesh: dp: 16 (over z, y, x), tensor: 2 (over core).
Axes of the slice: x: 2, y: 2, z: 4, core: 2. Of those that a mesh axis runs over, the one named last changes fastest.
Arguments:
- tokens: bfloat16 [16, 1024, 1024], P('dp', 'tensor'), may hold values from -6 to 6
- lengths: int32 [16], P('dp'), may hold values from 256 to 1024, as said below
- cotangent: bfloat16 [16, 1024, 1024], P('dp', 'tensor'), may hold values from -6 to 6
- query_key_value: float32 [1024, 3, 1024], P('dp', None, 'tensor'), may hold values from -0.1875 to 0.1875
- dense_weight: float32 [1024, 1024], P('dp', 'tensor'), may hold values from -0.75 to 0.75
- expand_weight: float32 [4096, 1024], P(('dp', 'tensor')), may hold values from -0.1875 to 0.1875
- shrink_weight: float32 [4096, 1024], P(('dp', 'tensor')), may hold values from -0.09375 to 0.09375
- query_value_bias: float32 [2, 1024], P(None, 'tensor'), may hold values from -1.8 to 1.8
- expand_bias: float32 [4096], P(('dp', 'tensor')), may hold values from -1.8 to 1.8
- small_params: float32 [6, 1024], P(None, ('dp', 'tensor')), may hold values from -1.5 to 1.5, as said below
- query_key_value_moment: float32 [1024, 3, 1024], P('dp', None, 'tensor'), may hold values from -23.04 to 23.04
- dense_moment: float32 [1024, 1024], P('dp', 'tensor'), may hold values from -23.04 to 23.04
- expand_moment: float32 [4096, 1024], P(('dp', 'tensor')), may hold values from -23.04 to 23.04
- shrink_moment: float32 [4096, 1024], P(('dp', 'tensor')), may hold values from -23.04 to 23.04
- small_first: float32 [6, 1024], P(None, ('dp', 'tensor')), may hold values from -7.68 to 7.68
- small_second: float32 [6, 1024], P(None, ('dp', 'tensor')), may hold values from 1.6384 to 16.384
- bias_first: float32 [2, 1024], P(None, 'tensor'), may hold values from -7.68 to 7.68
- bias_second: float32 [2, 1024], P(None, 'tensor'), may hold values from 1.6384 to 16.384
- expand_first: float32 [4096], P(('dp', 'tensor')), may hold values from -7.68 to 7.68
- expand_second: float32 [4096], P(('dp', 'tensor')), may hold values from 1.6384 to 16.384
- step_count: int32 [1], replicated, may hold values from 1 to 3
Outputs:
- output: bfloat16 [16, 1024, 1024], P('dp', 'tensor')
- input_grad: float32 [16, 1024, 1024], P('dp', 'tensor')
- query_key_value_grad: float32 [1024, 3, 1024], P('dp', None, 'tensor')
- dense_grad: float32 [1024, 1024], P('dp', 'tensor')
- expand_grad: float32 [4096, 1024], P(('dp', 'tensor'))
- shrink_grad: float32 [4096, 1024], P(('dp', 'tensor'))
- query_value_bias_grad: float32 [2, 1024], P(None, 'tensor')
- expand_bias_grad: float32 [4096], P(('dp', 'tensor'))
- small_params_grad: float32 [6, 1024], P(None, ('dp', 'tensor'))
- query_key_value_new: float32 [1024, 3, 1024], P('dp', None, 'tensor')
- dense_new: float32 [1024, 1024], P('dp', 'tensor')
- expand_new: float32 [4096, 1024], P(('dp', 'tensor'))
- shrink_new: float32 [4096, 1024], P(('dp', 'tensor'))
- query_value_bias_new: float32 [2, 1024], P(None, 'tensor')
- expand_bias_new: float32 [4096], P(('dp', 'tensor'))
- small_params_new: float32 [6, 1024], P(None, ('dp', 'tensor'))
- query_key_value_moment_new: float32 [1024, 3, 1024], P('dp', None, 'tensor')
- dense_moment_new: float32 [1024, 1024], P('dp', 'tensor')
- expand_moment_new: float32 [4096, 1024], P(('dp', 'tensor'))
- shrink_moment_new: float32 [4096, 1024], P(('dp', 'tensor'))
- small_first_new: float32 [6, 1024], P(None, ('dp', 'tensor'))
- small_second_new: float32 [6, 1024], P(None, ('dp', 'tensor'))
- bias_first_new: float32 [2, 1024], P(None, 'tensor')
- bias_second_new: float32 [2, 1024], P(None, 'tensor')
- expand_first_new: float32 [4096], P(('dp', 'tensor'))
- expand_second_new: float32 [4096], P(('dp', 'tensor'))
The draws below stay inside these ranges and needn't reach their ends.
Inputs may be any that keep to these rules, and one draw needn't show every extreme that they name: `lengths`: in every draw one sequence has 1024 valid positions and another a quarter of 1024. `small_params`: rows 0 and 3 lie within 0.5 to 1.5.
All inputs are finite; a program needn't handle non-finite values.
Results may differ from the reference program's by a relative error of at most 0.012.
The reference program's roundings to bfloat16 on the way count: a program that leaves them out, or rounds other values in their place, can miss the bound.
Values may be sent and summed in bfloat16 or wider, within the bound.
No kernel may reach another device: no remote copies, remote signals or barrier semaphores. Data moves between devices by JAX's collectives and lax.ppermute only.
A program may use at most 192 MiB of HBM per device.

```python
import math
import jax
import jax.numpy as jnp
from jax import lax

D = 1024
H = 16
HD = 64
FF = 4096
PAD = 1024
SEQS = 16
TOKENS = 16384
QBLOCK = 512


def draw_lengths(key, part):
    first, second = jax.random.split(key)
    drawn = jax.random.randint(first, (SEQS,), PAD // 4, PAD + 1, dtype=jnp.int32)
    order = jax.random.permutation(second, SEQS)
    drawn = drawn.at[order[0]].set(PAD)
    drawn = drawn.at[order[1]].set(PAD // 4)
    return drawn.astype(jnp.int32)


def draw_small_params(key, part):
    noise = jnp.clip(jax.random.normal(key, (6, D), jnp.float32), -5.0, 5.0)
    gains = jnp.array([1.0, 0.0, 0.0, 1.0, 0.0, 0.0], jnp.float32)[:, None]
    return gains * (1.0 + 0.1 * noise) + (1.0 - gains) * (0.3 * noise)


def steps_of(rng, shape, cuts, low, largest):
    loudness = 1.0
    for position, parts in cuts:
        steps = jax.random.uniform(jax.random.fold_in(jax.random.fold_in(rng, 6), position), (parts,), jnp.float32, low / len(cuts), largest / len(cuts))
        loudness = loudness * jnp.repeat(jnp.exp(steps), shape[position] // parts).reshape((-1,) + (1,) * (len(shape) - 1 - position))
    return loudness


def normal_values(key, shape, spread, limit, cuts=(), kind=jnp.bfloat16):
    values = jax.random.normal(key, shape, jnp.float32) * spread
    if len(cuts) > 0:
        values = steps_of(key, shape, cuts, -0.22, 0.18) * values
    return jnp.clip(values, min=-limit, max=limit).astype(kind)


def setup_inputs(seed: int = 0) -> dict:
    seeds = jax.random.split(jax.random.key(seed), 22)
    return {
        "tokens": normal_values(seeds[0], (SEQS, PAD, D), 1.0, 6.0, ((0, 16), (1, 2))),
        "lengths": draw_lengths(jax.random.fold_in(seeds[21], 71), 0),
        "cotangent": normal_values(seeds[2], (SEQS, PAD, D), 1.0, 6.0, ((0, 16), (1, 2))),
        "query_key_value": normal_values(seeds[3], (D, 3, D), D ** -0.5, 0.1875, ((0, 16), (2, 2)), jnp.float32),
        "dense_weight": normal_values(seeds[4], (D, D), HD ** -0.5, 0.75, ((0, 16), (1, 2)), jnp.float32),
        "expand_weight": normal_values(seeds[5], (FF, D), D ** -0.5, 0.1875, ((0, 32),), jnp.float32),
        "shrink_weight": normal_values(seeds[6], (FF, D), FF ** -0.5, 0.09375, ((0, 32),), jnp.float32),
        "query_value_bias": normal_values(seeds[7], (2, D), 0.3, 1.8, ((1, 2),), jnp.float32),
        "expand_bias": normal_values(seeds[8], (FF,), 0.3, 1.8, ((0, 32),), jnp.float32),
        "small_params": draw_small_params(jax.random.fold_in(seeds[21], 71), 0),
        "query_key_value_moment": normal_values(seeds[10], (D, 3, D), (0.03 * TOKENS ** 0.5), 23.04, ((0, 16), (2, 2)), jnp.float32),
        "dense_moment": normal_values(seeds[11], (D, D), (0.03 * TOKENS ** 0.5), 23.04, ((0, 16), (1, 2)), jnp.float32),
        "expand_moment": normal_values(seeds[12], (FF, D), (0.03 * TOKENS ** 0.5), 23.04, ((0, 32),), jnp.float32),
        "shrink_moment": normal_values(seeds[13], (FF, D), (0.03 * TOKENS ** 0.5), 23.04, ((0, 32),), jnp.float32),
        "small_first": normal_values(seeds[14], (6, D), (0.01 * TOKENS ** 0.5), 7.68, ((1, 32),), jnp.float32),
        "small_second": jnp.clip(jnp.exp(math.log(16.384) - 2.3025852 * jax.random.uniform(seeds[15], (6, D), jnp.float32) ** steps_of(seeds[15], (6, D), ((1, 32),), -0.2, 0.2)), 1.6384, 16.384),
        "bias_first": normal_values(seeds[16], (2, D), (0.01 * TOKENS ** 0.5), 7.68, ((1, 2),), jnp.float32),
        "bias_second": jnp.clip(jnp.exp(math.log(16.384) - 2.3025852 * jax.random.uniform(seeds[17], (2, D), jnp.float32) ** steps_of(seeds[17], (2, D), ((1, 2),), -0.2, 0.2)), 1.6384, 16.384),
        "expand_first": normal_values(seeds[18], (FF,), (0.01 * TOKENS ** 0.5), 7.68, ((0, 32),), jnp.float32),
        "expand_second": jnp.clip(jnp.exp(math.log(16.384) - 2.3025852 * jax.random.uniform(seeds[19], (FF,), jnp.float32) ** steps_of(seeds[19], (FF,), ((0, 32),), -0.2, 0.2)), 1.6384, 16.384),
        "step_count": jax.random.randint(seeds[20], (1,), 1, 4).astype(jnp.int32),
    }


@jax.custom_vjp
def low(v):
    return lax.optimization_barrier(v.astype(jnp.bfloat16)).astype(jnp.float32)

@jax.custom_vjp
def low_back(v):
    return v

def low_keep(v):
    return (low(v), None)

def low_pass(kept, grad):
    return (grad,)

def back_keep(v):
    return (v, None)

def back_low(kept, grad):
    return (low(grad),)
low.defvjp(low_keep, low_pass)
low_back.defvjp(back_keep, back_low)
layer_eps = 1e-05
muon_eps = 1e-07
adam_eps = 1e-08
decay_rate = 0.95
muon_rate = 0.25
adam_rate = 0.2
beta_first = 0.9
beta_second = 0.999
first_coef = 3.4445
second_coef = -4.775
third_coef = 2.0315
highest = lax.Precision.HIGHEST

def normalize(values):
    centered = values - lax.optimization_barrier(jnp.mean(values, axis=-1, keepdims=True))
    return centered * lax.rsqrt(lax.optimization_barrier(jnp.mean(centered * centered, axis=-1, keepdims=True)) + layer_eps)

def attention(queries, keys, values, length):
    head_rows = queries.reshape(PAD, H, HD)
    key_rows = keys.reshape(PAD, H, HD)
    value_rows = values.reshape(PAD, H, HD)
    slopes = jnp.exp2(-8.0 * (jnp.arange(H, dtype=jnp.int32) + 1).astype(jnp.float32) / H)
    columns = jnp.arange(PAD, dtype=jnp.int32)

    def one(begin):
        query_block = lax.dynamic_slice_in_dim(head_rows, begin.astype(jnp.int32), QBLOCK, 0)
        rows = begin.astype(jnp.int32) + jnp.arange(QBLOCK, dtype=jnp.int32)
        scores = jnp.einsum('qhc,khc->hqk', query_block, key_rows, precision=highest) * HD ** (-0.5)
        offset = (rows[:, None] - columns[None, :]).astype(jnp.float32)
        allowed = (columns[None, :] <= rows[:, None]) & (columns[None, :] < length)
        scores = low_back(jnp.where(allowed[None], scores - slopes[:, None, None] * offset[None], -1e+30))
        probs = jax.nn.softmax(scores, axis=-1)
        return jnp.einsum('hqk,khc->qhc', low(probs), value_rows, precision=highest)
    starts = jnp.arange(0, PAD, QBLOCK, dtype=jnp.int32)
    mixed = lax.map(jax.checkpoint(one), starts)
    return mixed.reshape(PAD, D)

def sequence(inputs, length, weights):
    triple, dense, expand, shrink, query_shift, expand_shift, small = weights
    positions = jnp.arange(PAD, dtype=jnp.int32)
    hidden_one = low(normalize(inputs) * small[0] + small[1])
    projected = jnp.einsum('sd,dkc->skc', hidden_one, triple, precision=highest)
    queries = low(low_back(projected[:, 0] + query_shift[0]))
    keys = low(low_back(projected[:, 1]))
    values = low(low_back(projected[:, 2] + query_shift[1]))
    mixed = low(low_back(attention(queries, keys, values, length)))
    residual = inputs + low_back(jnp.dot(mixed, dense.T, precision=highest) + small[2])
    hidden_two = low(normalize(residual) * small[3] + small[4])
    expanded = low_back(jnp.dot(hidden_two, expand.T, precision=highest) + expand_shift)
    activated = low(jax.nn.gelu(expanded, approximate=True))
    result = residual + low_back(jnp.dot(activated, shrink, precision=highest) + small[5])
    return jnp.where((positions < length)[:, None], result, 0.0)

def orthogonalize(update):
    scale = jnp.sqrt(lax.optimization_barrier(jnp.sum(update * update, axis=(1, 2), keepdims=True))) + muon_eps
    ortho = update / scale
    for turn in range(5):
        gram = jnp.einsum('bri,brj->bij', ortho, ortho, precision=highest)
        product = jnp.einsum('brj,bjk->brk', ortho, gram, precision=highest)
        twice = jnp.einsum('brj,bjk->brk', product, gram, precision=highest)
        ortho = first_coef * ortho + second_coef * product + third_coef * twice
    return ortho

def adam_step(param, gradient, first, second, count):
    first_new = beta_first * first + (1.0 - beta_first) * gradient
    second_new = beta_second * second + (1.0 - beta_second) * gradient * gradient
    corr_one = 1.0 - jnp.power(beta_first, count)
    corr_two = 1.0 - jnp.power(beta_second, count)
    change = adam_rate * (first_new / corr_one) / (jnp.sqrt(second_new / corr_two) + adam_eps)
    return (param - change, first_new, second_new)

def reference(tokens, lengths, cotangent, query_key_value, dense_weight, expand_weight, shrink_weight, query_value_bias, expand_bias, small_params, query_key_value_moment, dense_moment, expand_moment, shrink_moment, small_first, small_second, bias_first, bias_second, expand_first, expand_second, step_count):

    def forward(triple, dense, expand, shrink, query_shift, expand_shift, small, inputs):
        weights = (low(triple), low(dense), low(expand), low(shrink), low(query_shift), low(expand_shift), low(small))

        def one(pair):
            return sequence(pair[0], pair[1], weights)
        return lax.map(jax.checkpoint(one), (inputs, lengths))
    result, pull = jax.vjp(forward, query_key_value, dense_weight, expand_weight, shrink_weight, query_value_bias, expand_bias, small_params, tokens.astype(jnp.float32))
    triple_grad, dense_grad, expand_grad, shrink_grad, bias_grad, shift_grad, small_grad, input_grad = pull(cotangent.astype(jnp.float32))
    count = step_count[0].astype(jnp.float32)
    triple_moment = decay_rate * query_key_value_moment + triple_grad
    dense_moment_new = decay_rate * dense_moment + dense_grad
    expand_moment_new = decay_rate * expand_moment + expand_grad
    shrink_moment_new = decay_rate * shrink_moment + shrink_grad
    head_update = jnp.concatenate(((triple_grad + decay_rate * triple_moment).reshape(D, 3 * H, HD).transpose(1, 0, 2), (dense_grad + decay_rate * dense_moment_new).reshape(D, H, HD).transpose(1, 0, 2)), axis=0)
    head_change = orthogonalize(head_update) * (muon_rate * math.sqrt(max(1.0, D / HD)))
    triple_new = query_key_value - head_change[:3 * H].transpose(1, 0, 2).reshape(D, 3, D)
    dense_new = dense_weight - head_change[3 * H:].transpose(1, 0, 2).reshape(D, D)
    feed_blocks = D // HD
    feed_update = jnp.stack((expand_grad + decay_rate * expand_moment_new, shrink_grad + decay_rate * shrink_moment_new))
    feed_update = feed_update.reshape(2, FF, feed_blocks, HD).transpose(0, 2, 1, 3).reshape(2 * feed_blocks, FF, HD)
    feed_change = orthogonalize(feed_update) * (muon_rate * math.sqrt(max(1.0, FF / HD)))
    feed_change = feed_change.reshape(2, feed_blocks, FF, HD).transpose(0, 2, 1, 3).reshape(2, FF, D)
    expand_new = expand_weight - feed_change[0]
    shrink_new = shrink_weight - feed_change[1]
    small_new, small_first_new, small_second_new = adam_step(small_params, small_grad, small_first, small_second, count)
    bias_new, bias_first_new, bias_second_new = adam_step(query_value_bias, bias_grad, bias_first, bias_second, count)
    shift_new, expand_first_new, expand_second_new = adam_step(expand_bias, shift_grad, expand_first, expand_second, count)
    return (result.astype(jnp.bfloat16), input_grad, triple_grad, dense_grad, expand_grad, shrink_grad, bias_grad, shift_grad, small_grad, triple_new, dense_new, expand_new, shrink_new, bias_new, shift_new, small_new, triple_moment, dense_moment_new, expand_moment_new, shrink_moment_new, small_first_new, small_second_new, bias_first_new, bias_second_new, expand_first_new, expand_second_new)
```

```python
import math

import jax
import jax.numpy as jnp
from jax import lax
from jax.sharding import PartitionSpec as P

H = 16
HD = 64
FF = 4096


layer_eps = 1e-05
muon_eps = 1e-07
adam_eps = 1e-08
decay_rate = 0.95
muon_rate = 0.25
adam_rate = 0.2
beta_first = 0.9
beta_second = 0.999
first_coef = 3.4445
second_coef = -4.775
third_coef = 2.0315
highest = lax.Precision.HIGHEST
contract_last = (((1,), (1,)), ((), ()))
contract_first = (((0,), (0,)), ((), ()))


def normalize(values):
    centered = values - jnp.mean(values, axis=-1, keepdims=True)
    inverse = lax.rsqrt(jnp.mean(centered * centered, axis=-1, keepdims=True) + layer_eps)
    return (centered * inverse, inverse)


def norm_back(upstream, normed, inverse, gain):
    scaled = upstream * gain
    return inverse * (
        scaled
        - jnp.mean(scaled, axis=-1, keepdims=True)
        - normed * jnp.mean(scaled * normed, axis=-1, keepdims=True)
    )


def gelu_slope(values):
    inner = jnp.tanh(0.7978845608028654 * (values + 0.044715 * values**3))
    return 0.5 * (1.0 + inner) + 0.5 * values * (1.0 - inner * inner) * 0.7978845608028654 * (
        1.0 + 3.0 * 0.044715 * values * values
    )


def score_block(query_block, keys, rows, length, slopes):
    scores = jnp.einsum(
        "qhc,khc->hqk", query_block, keys, preferred_element_type=jnp.float32
    ) * keys.shape[-1] ** (-0.5)
    columns = jnp.arange(keys.shape[0], dtype=jnp.int32)
    offset = (rows[:, None] - columns[None, :]).astype(jnp.float32)
    allowed = (columns[None, :] <= rows[:, None]) & (columns[None, :] < length)
    return jnp.where(allowed[None], scores - slopes[:, None, None] * offset[None], -1e30)


def attend(queries, keys, values, length, slopes, block):
    count = queries.shape[0] // block

    def one(index):
        begin = index * block
        query_block = lax.dynamic_slice_in_dim(queries, begin, block, 0)
        rows = begin + jnp.arange(block, dtype=jnp.int32)
        scores = score_block(query_block, keys, rows, length, slopes)
        peak = jnp.max(scores, axis=-1, keepdims=True)
        weights = jnp.exp(scores - peak)
        total = jnp.sum(weights, axis=-1, keepdims=True)
        mixed = jnp.einsum(
            "hqk,khc->qhc",
            (weights / total).astype(jnp.bfloat16),
            values,
            preferred_element_type=jnp.float32,
        )
        return (mixed.astype(jnp.bfloat16), (peak + jnp.log(total))[:, :, 0])

    mixed, logsum = lax.map(one, jnp.arange(count, dtype=jnp.int32))
    return (mixed.reshape(queries.shape), logsum)


def attend_back(queries, keys, values, grad_mixed, logsum, length, slopes, block):
    count = queries.shape[0] // block
    scale = queries.shape[-1] ** (-0.5)

    def one(carry, index):
        key_total, value_total = carry
        begin = index * block
        query_block = lax.dynamic_slice_in_dim(queries, begin, block, 0)
        grad_block = lax.dynamic_slice_in_dim(grad_mixed, begin, block, 0)
        rows = begin + jnp.arange(block, dtype=jnp.int32)
        scores = score_block(query_block, keys, rows, length, slopes)
        probs = jnp.exp(scores - logsum[index][:, :, None])
        grad_probs = jnp.einsum(
            "qhc,khc->hqk", grad_block, values, preferred_element_type=jnp.float32
        )
        inner = jnp.sum(probs * grad_probs, axis=-1, keepdims=True)
        grad_scores = (probs * (grad_probs - inner)).astype(jnp.bfloat16)
        grad_query = (
            jnp.einsum("hqk,khc->qhc", grad_scores, keys, preferred_element_type=jnp.float32)
            * scale
        )
        key_total = (
            key_total
            + jnp.einsum(
                "hqk,qhc->khc", grad_scores, query_block, preferred_element_type=jnp.float32
            )
            * scale
        )
        value_total = value_total + jnp.einsum(
            "hqk,qhc->khc",
            probs.astype(jnp.bfloat16),
            grad_block,
            preferred_element_type=jnp.float32,
        )
        return ((key_total, value_total), grad_query.astype(jnp.bfloat16))

    empty = jnp.zeros(keys.shape, jnp.float32)
    (key_total, value_total), grad_query = lax.scan(
        one, (empty, empty), jnp.arange(count, dtype=jnp.int32)
    )
    return (
        grad_query.reshape(queries.shape),
        key_total.astype(jnp.bfloat16),
        value_total.astype(jnp.bfloat16),
    )


def block_gram(ortho):
    return jnp.einsum("rbi,rbj->bij", ortho, ortho, precision=highest)


def small_dot(left, right):
    return jnp.einsum("bij,bjk->bik", left, right, precision=highest)


def gram_factor(raw):
    scale = jnp.sqrt(jnp.trace(raw, axis1=1, axis2=2)) + muon_eps
    eye = jnp.eye(raw.shape[-1], dtype=jnp.float32)[None]
    gram = raw / (scale * scale)[:, None, None]
    factor = None
    for turn in range(5):
        step = first_coef * eye + second_coef * gram + third_coef * small_dot(gram, gram)
        factor = step if factor is None else small_dot(factor, step)
        if turn < 4:
            gram = small_dot(step, small_dot(gram, step))
    return factor / scale[:, None, None]


def shared_factor(partial, axes):
    count = partial.shape[0]
    parts = lax.axis_size(axes)
    extra = -count % parts
    if extra:
        partial = jnp.pad(partial, ((0, extra), (0, 0), (0, 0)))
    raw = lax.psum_scatter(partial, axes, scatter_dimension=0, tiled=True)
    factor = lax.all_gather(gram_factor(raw), axes, axis=0, tiled=True)
    return factor[:count]


def adam_step(param, gradient, first, second, count):
    first_new = beta_first * first + (1.0 - beta_first) * gradient
    second_new = beta_second * second + (1.0 - beta_second) * gradient * gradient
    corr_one = 1.0 - jnp.power(beta_first, count)
    corr_two = 1.0 - jnp.power(beta_second, count)
    change = adam_rate * (first_new / corr_one) / (jnp.sqrt(second_new / corr_two) + adam_eps)
    return (param - change, first_new, second_new)


def per_device(
    tokens,
    lengths,
    cotangent,
    query_key_value,
    dense_weight,
    expand_weight,
    shrink_weight,
    query_value_bias,
    expand_bias,
    small_params,
    query_key_value_moment,
    dense_moment,
    expand_moment,
    shrink_moment,
    small_first,
    small_second,
    bias_first,
    bias_second,
    expand_first,
    expand_second,
    step_count,
):
    pieces = lax.axis_size("tensor")
    local_rows = tokens.shape[1]
    seq_rows = local_rows * pieces
    width = tokens.shape[2]
    head_cols = query_key_value.shape[2]
    heads_here = head_cols // HD
    block = min(512, seq_rows)
    length = lengths[0]
    here = lax.axis_index("tensor")
    positions = here * local_rows + jnp.arange(local_rows, dtype=jnp.int32)
    valid = (positions < length).astype(jnp.float32)[:, None]
    head_index = here * heads_here + jnp.arange(heads_here, dtype=jnp.int32) + 1
    slopes = jnp.exp2(-8.0 * head_index.astype(jnp.float32) / H)
    low_triple = query_key_value.astype(jnp.bfloat16)
    low_dense = dense_weight.astype(jnp.bfloat16)
    low_expand = expand_weight.astype(jnp.bfloat16)
    low_shrink = shrink_weight.astype(jnp.bfloat16)
    low_shift = expand_bias.astype(jnp.bfloat16)
    low_small = small_params.astype(jnp.bfloat16)
    other_small = lax.ppermute(
        low_small, "tensor", [(i, (i + 1) % pieces) for i in range(pieces)]
    )
    pair_small = jnp.where(
        here == 0,
        jnp.concatenate((low_small, other_small), axis=1),
        jnp.concatenate((other_small, low_small), axis=1),
    )
    extras = jnp.concatenate((low_shift, pair_small.reshape(-1)))
    extra_rows = -(-extras.shape[0] // head_cols)
    extras = jnp.pad(extras, (0, extra_rows * head_cols - extras.shape[0]))
    dense_rows = low_dense.shape[0]
    packed = lax.all_gather(
        jnp.concatenate((low_dense, extras.reshape(extra_rows, head_cols)), axis=0), "dp", axis=0
    )
    groups = packed.shape[0]
    dense = packed[:, :dense_rows].reshape(groups * dense_rows, head_cols)
    packed_extras = packed[:, dense_rows:].reshape(groups, extra_rows * head_cols)
    shifts = low_shift.shape[0]
    expand_shift = packed_extras[:, :shifts].reshape(-1)
    smalls = pair_small.size
    small = (
        packed_extras[:, shifts : shifts + smalls]
        .reshape((groups,) + pair_small.shape)
        .transpose(1, 0, 2)
        .reshape(pair_small.shape[0], width)
        .astype(jnp.float32)
    )
    triple, expand, shrink = (
        lax.all_gather(low_triple, "dp", axis=0, tiled=True),
        lax.all_gather(low_expand, "dp", axis=0, tiled=True),
        lax.all_gather(low_shrink, "dp", axis=0, tiled=True),
    )
    query_shift = lax.optimization_barrier(query_value_bias.astype(jnp.bfloat16)).astype(
        jnp.float32
    )
    shift_values = expand_shift.astype(jnp.float32)
    inputs = tokens[0].astype(jnp.float32)
    normed_one, inverse_one = normalize(inputs)
    hidden_one = lax.all_gather(
        (normed_one * small[0] + small[1]).astype(jnp.bfloat16), "tensor", axis=0, tiled=True
    )
    projected = jnp.einsum("sd,dkc->skc", hidden_one, triple, preferred_element_type=jnp.float32)
    queries = (
        (projected[:, 0] + query_shift[0]).astype(jnp.bfloat16).reshape(seq_rows, heads_here, HD)
    )
    keys = projected[:, 1].astype(jnp.bfloat16).reshape(seq_rows, heads_here, HD)
    values = (
        (projected[:, 2] + query_shift[1]).astype(jnp.bfloat16).reshape(seq_rows, heads_here, HD)
    )
    mixed, logsum = attend(queries, keys, values, length, slopes, block)
    mixed_flat = mixed.reshape(seq_rows, head_cols)
    residual = inputs + (
        lax.psum_scatter(
            lax.dot_general(mixed_flat, dense, contract_last, preferred_element_type=jnp.float32),
            "tensor",
            scatter_dimension=0,
            tiled=True,
        )
        + small[2]
    )
    normed_two, inverse_two = normalize(residual)
    hidden_local = (normed_two * small[3] + small[4]).astype(jnp.bfloat16)
    grad_result = valid * cotangent[0].astype(jnp.float32)
    grad_feed = grad_result.astype(jnp.bfloat16)
    hidden_two = lax.all_gather(hidden_local, "tensor", axis=0, tiled=True)
    expanded = (
        lax.dot_general(hidden_two, expand, contract_last, preferred_element_type=jnp.float32)
        + shift_values
    )
    activated = jax.nn.gelu(expanded, approximate=True).astype(jnp.bfloat16)
    feed = lax.psum_scatter(
        jnp.dot(activated, shrink, preferred_element_type=jnp.float32),
        "tensor",
        scatter_dimension=0,
        tiled=True,
    )
    grad_feed_all = lax.all_gather(grad_feed, "tensor", axis=0, tiled=True)
    grad_act = lax.dot_general(
        grad_feed_all, shrink, contract_last, preferred_element_type=jnp.float32
    )
    shrink_grad = lax.dot_general(
        activated, grad_feed_all, contract_first, preferred_element_type=jnp.float32
    )
    grad_expanded = (grad_act * gelu_slope(expanded)).astype(jnp.bfloat16)
    expand_grad = lax.dot_general(
        grad_expanded, hidden_two, contract_first, preferred_element_type=jnp.float32
    )
    grad_hidden_two = lax.psum_scatter(
        jnp.dot(grad_expanded, expand, preferred_element_type=jnp.float32),
        "tensor",
        scatter_dimension=0,
        tiled=True,
    )
    shift_grad = jnp.sum(grad_expanded.astype(jnp.float32), axis=0)
    output = (valid * (residual + (feed + small[5]))).astype(jnp.bfloat16)[None]
    grad_residual = grad_result + norm_back(grad_hidden_two, normed_two, inverse_two, small[3])
    grad_branch = grad_residual.astype(jnp.bfloat16)
    grad_branch_all = lax.all_gather(grad_branch, "tensor", axis=0, tiled=True)
    dense_grad = lax.dot_general(
        grad_branch_all, mixed_flat, contract_first, preferred_element_type=jnp.float32
    )
    grad_mixed = (
        jnp.dot(grad_branch_all, dense, preferred_element_type=jnp.float32)
        .astype(jnp.bfloat16)
        .reshape(seq_rows, heads_here, HD)
    )
    grad_queries, grad_keys, grad_values = attend_back(
        queries, keys, values, grad_mixed, logsum, length, slopes, block
    )
    grad_projected = jnp.stack((grad_queries, grad_keys, grad_values), axis=1).reshape(
        seq_rows, 3, head_cols
    )
    bias_grad_local = jnp.sum(grad_projected[:, 0::2].astype(jnp.float32), axis=0)
    triple_grad = jnp.einsum(
        "sd,skc->dkc", hidden_one, grad_projected, preferred_element_type=jnp.float32
    )
    grad_hidden_one = lax.psum_scatter(
        jnp.einsum("skc,dkc->sd", grad_projected, triple, preferred_element_type=jnp.float32),
        "tensor",
        scatter_dimension=0,
        tiled=True,
    )
    input_grad = grad_residual + norm_back(grad_hidden_one, normed_one, inverse_one, small[0])
    small_terms = jnp.stack(
        (
            jnp.sum(grad_hidden_one * normed_one, axis=0),
            jnp.sum(grad_hidden_one, axis=0),
            jnp.sum(grad_branch.astype(jnp.float32), axis=0),
            jnp.sum(grad_hidden_two * normed_two, axis=0),
            jnp.sum(grad_hidden_two, axis=0),
            jnp.sum(grad_feed.astype(jnp.float32), axis=0),
        )
    )
    small_grad = lax.psum_scatter(small_terms, ("dp", "tensor"), scatter_dimension=1, tiled=True)
    triple_sum, dense_sum, expand_sum, shrink_sum, shift_sum = (
        lax.psum_scatter(triple_grad, "dp", scatter_dimension=0, tiled=True),
        lax.psum_scatter(dense_grad, "dp", scatter_dimension=0, tiled=True),
        lax.psum_scatter(expand_grad, "dp", scatter_dimension=0, tiled=True),
        lax.psum_scatter(shrink_grad, "dp", scatter_dimension=0, tiled=True),
        lax.psum_scatter(shift_grad, "dp", scatter_dimension=0, tiled=True),
    )
    count = step_count[0].astype(jnp.float32)
    rows_here = triple_sum.shape[0]
    triple_moment = decay_rate * query_key_value_moment + triple_sum
    dense_moment_new = decay_rate * dense_moment + dense_sum
    expand_moment_new = decay_rate * expand_moment + expand_sum
    shrink_moment_new = decay_rate * shrink_moment + shrink_sum
    head_update = jnp.concatenate(
        (
            (triple_sum + decay_rate * triple_moment).reshape(rows_here, 3 * heads_here, HD),
            (dense_sum + decay_rate * dense_moment_new).reshape(rows_here, heads_here, HD),
        ),
        axis=1,
    )
    feed_rows = expand_sum.shape[0]
    feed_blocks = width // HD
    feed_update = jnp.stack(
        (expand_sum + decay_rate * expand_moment_new, shrink_sum + decay_rate * shrink_moment_new)
    )
    feed_update = (
        feed_update.reshape(2, feed_rows, feed_blocks, HD)
        .transpose(1, 0, 2, 3)
        .reshape(feed_rows, 2 * feed_blocks, HD)
    )
    bias_sum = lax.psum(bias_grad_local, "dp")
    head_factor = shared_factor(block_gram(head_update), "dp")
    feed_factor = shared_factor(block_gram(feed_update), ("dp", "tensor"))
    head_ortho = jnp.einsum("rbi,bij->rbj", head_update, head_factor, precision=highest)
    feed_ortho = jnp.einsum("rbi,bij->rbj", feed_update, feed_factor, precision=highest)
    head_change = head_ortho * (muon_rate * math.sqrt(max(1.0, width / HD)))
    triple_new = query_key_value - head_change[:, : 3 * heads_here].reshape(rows_here, 3, head_cols)
    dense_new = dense_weight - head_change[:, 3 * heads_here :].reshape(rows_here, head_cols)
    feed_change = feed_ortho * (muon_rate * math.sqrt(max(1.0, FF / HD)))
    feed_change = (
        feed_change.reshape(feed_rows, 2, feed_blocks, HD)
        .transpose(1, 0, 2, 3)
        .reshape(2, feed_rows, width)
    )
    expand_new = expand_weight - feed_change[0]
    shrink_new = shrink_weight - feed_change[1]
    small_new, small_first_new, small_second_new = adam_step(
        small_params, small_grad, small_first, small_second, count
    )
    bias_new, bias_first_new, bias_second_new = adam_step(
        query_value_bias, bias_sum, bias_first, bias_second, count
    )
    shift_new, expand_first_new, expand_second_new = adam_step(
        expand_bias, shift_sum, expand_first, expand_second, count
    )
    return (
        output,
        input_grad[None],
        triple_sum,
        dense_sum,
        expand_sum,
        shrink_sum,
        bias_sum,
        shift_sum,
        small_grad,
        triple_new,
        dense_new,
        expand_new,
        shrink_new,
        bias_new,
        shift_new,
        small_new,
        triple_moment,
        dense_moment_new,
        expand_moment_new,
        shrink_moment_new,
        small_first_new,
        small_second_new,
        bias_first_new,
        bias_second_new,
        expand_first_new,
        expand_second_new,
    )


def solution(mesh):
    in_specs = (
        P("dp", "tensor", None),
        P("dp"),
        P("dp", "tensor", None),
        P("dp", None, "tensor"),
        P("dp", "tensor"),
        P(("dp", "tensor"), None),
        P(("dp", "tensor"), None),
        P(None, "tensor"),
        P(("dp", "tensor")),
        P(None, ("dp", "tensor")),
        P("dp", None, "tensor"),
        P("dp", "tensor"),
        P(("dp", "tensor"), None),
        P(("dp", "tensor"), None),
        P(None, ("dp", "tensor")),
        P(None, ("dp", "tensor")),
        P(None, "tensor"),
        P(None, "tensor"),
        P(("dp", "tensor")),
        P(("dp", "tensor")),
        P(),
    )
    out_specs = (
        P("dp", "tensor", None),
        P("dp", "tensor", None),
        P("dp", None, "tensor"),
        P("dp", "tensor"),
        P(("dp", "tensor"), None),
        P(("dp", "tensor"), None),
        P(None, "tensor"),
        P(("dp", "tensor")),
        P(None, ("dp", "tensor")),
        P("dp", None, "tensor"),
        P("dp", "tensor"),
        P(("dp", "tensor"), None),
        P(("dp", "tensor"), None),
        P(None, "tensor"),
        P(("dp", "tensor")),
        P(None, ("dp", "tensor")),
        P("dp", None, "tensor"),
        P("dp", "tensor"),
        P(("dp", "tensor"), None),
        P(("dp", "tensor"), None),
        P(None, ("dp", "tensor")),
        P(None, ("dp", "tensor")),
        P(None, "tensor"),
        P(None, "tensor"),
        P(("dp", "tensor")),
        P(("dp", "tensor")),
    )
    return jax.shard_map(
        per_device, mesh=mesh, in_specs=in_specs, out_specs=out_specs, check_vma=False
    )
```

```python
import math

import jax
import jax.numpy as jnp
from jax import lax
from jax.sharding import PartitionSpec as P

H = 16
HD = 64
FF = 4096


layer_eps = 1e-05
muon_eps = 1e-07
adam_eps = 1e-08
decay_rate = 0.95
muon_rate = 0.25
adam_rate = 0.2
beta_first = 0.9
beta_second = 0.999
first_coef = 3.4445
second_coef = -4.775
third_coef = 2.0315
highest = lax.Precision.HIGHEST
contract_last = (((1,), (1,)), ((), ()))
contract_first = (((0,), (0,)), ((), ()))


def normalize(values):
    centered = values - jnp.mean(values, axis=-1, keepdims=True)
    inverse = lax.rsqrt(jnp.mean(centered * centered, axis=-1, keepdims=True) + layer_eps)
    return (centered * inverse, inverse)


def norm_back(upstream, normed, inverse, gain):
    scaled = upstream * gain
    return inverse * (
        scaled
        - jnp.mean(scaled, axis=-1, keepdims=True)
        - normed * jnp.mean(scaled * normed, axis=-1, keepdims=True)
    )


def gelu_slope(values):
    inner = jnp.tanh(0.7978845608028654 * (values + 0.044715 * values**3))
    return 0.5 * (1.0 + inner) + 0.5 * values * (1.0 - inner * inner) * 0.7978845608028654 * (
        1.0 + 3.0 * 0.044715 * values * values
    )


def score_block(query_block, keys, rows, length, slopes):
    scores = jnp.einsum(
        "qhc,khc->hqk", query_block, keys, preferred_element_type=jnp.float32
    ) * keys.shape[-1] ** (-0.5)
    columns = jnp.arange(keys.shape[0], dtype=jnp.int32)
    offset = (rows[:, None] - columns[None, :]).astype(jnp.float32)
    allowed = (columns[None, :] <= rows[:, None]) & (columns[None, :] < length)
    return jnp.where(allowed[None], scores - slopes[:, None, None] * offset[None], -1e30)


def attend(queries, keys, values, length, slopes, block):
    count = queries.shape[0] // block

    def one(index):
        begin = index * block
        query_block = lax.dynamic_slice_in_dim(queries, begin, block, 0)
        rows = begin + jnp.arange(block, dtype=jnp.int32)
        scores = score_block(query_block, keys, rows, length, slopes)
        peak = jnp.max(scores, axis=-1, keepdims=True)
        weights = jnp.exp(scores - peak)
        total = jnp.sum(weights, axis=-1, keepdims=True)
        mixed = jnp.einsum(
            "hqk,khc->qhc",
            (weights / total).astype(jnp.bfloat16),
            values,
            preferred_element_type=jnp.float32,
        )
        return (mixed.astype(jnp.bfloat16), (peak + jnp.log(total))[:, :, 0])

    mixed, logsum = lax.map(one, jnp.arange(count, dtype=jnp.int32))
    return (mixed.reshape(queries.shape), logsum)


def attend_back(queries, keys, values, grad_mixed, logsum, length, slopes, block):
    count = queries.shape[0] // block
    scale = queries.shape[-1] ** (-0.5)

    def one(carry, index):
        key_total, value_total = carry
        begin = index * block
        query_block = lax.dynamic_slice_in_dim(queries, begin, block, 0)
        grad_block = lax.dynamic_slice_in_dim(grad_mixed, begin, block, 0)
        rows = begin + jnp.arange(block, dtype=jnp.int32)
        scores = score_block(query_block, keys, rows, length, slopes)
        probs = jnp.exp(scores - logsum[index][:, :, None])
        grad_probs = jnp.einsum(
            "qhc,khc->hqk", grad_block, values, preferred_element_type=jnp.float32
        )
        inner = jnp.sum(probs * grad_probs, axis=-1, keepdims=True)
        grad_scores = (probs * (grad_probs - inner)).astype(jnp.bfloat16)
        grad_query = (
            jnp.einsum("hqk,khc->qhc", grad_scores, keys, preferred_element_type=jnp.float32)
            * scale
        )
        key_total = (
            key_total
            + jnp.einsum(
                "hqk,qhc->khc", grad_scores, query_block, preferred_element_type=jnp.float32
            )
            * scale
        )
        value_total = value_total + jnp.einsum(
            "hqk,qhc->khc",
            probs.astype(jnp.bfloat16),
            grad_block,
            preferred_element_type=jnp.float32,
        )
        return ((key_total, value_total), grad_query.astype(jnp.bfloat16))

    empty = jnp.zeros(keys.shape, jnp.float32)
    (key_total, value_total), grad_query = lax.scan(
        one, (empty, empty), jnp.arange(count, dtype=jnp.int32)
    )
    return (
        grad_query.reshape(queries.shape),
        key_total.astype(jnp.bfloat16),
        value_total.astype(jnp.bfloat16),
    )


def block_gram(ortho):
    return jnp.einsum("rbi,rbj->bij", ortho, ortho, precision=highest)


def small_dot(left, right):
    return jnp.einsum("bij,bjk->bik", left, right, precision=highest)


def gram_factor(raw):
    scale = jnp.sqrt(jnp.trace(raw, axis1=1, axis2=2)) + muon_eps
    eye = jnp.eye(raw.shape[-1], dtype=jnp.float32)[None]
    gram = raw / (scale * scale)[:, None, None]
    factor = None
    for turn in range(5):
        step = first_coef * eye + second_coef * gram + third_coef * small_dot(gram, gram)
        factor = step if factor is None else small_dot(factor, step)
        if turn < 4:
            gram = small_dot(step, small_dot(gram, step))
    return factor / scale[:, None, None]


def bits_of(parts):
    return max(parts.bit_length() - 1, 0)


def orders(parts):
    down = tuple(range(bits_of(parts)))[::-1]
    return (down, down[:-2] + (down[-1], down[-2]), (0, 1) + down[:-2])


def swap(values, bit, parts):
    return lax.ppermute(values, "dp", [(i, i ^ (1 << bit)) for i in range(parts)])


def own_bit(bit):
    return (lax.axis_index("dp") >> bit) & 1


def gather_bits(values, order, parts):
    count = bits_of(parts)
    held = values.reshape((1,) * count + values.shape)
    for bit in order:
        other = swap(held, bit, parts)
        axis = count - 1 - bit
        held = jnp.where(
            own_bit(bit) == 0,
            jnp.concatenate((held, other), axis),
            jnp.concatenate((other, held), axis),
        )
    return held.reshape((parts,) + values.shape)


def scatter_bits(values, order, parts, wire):
    count = bits_of(parts)
    held = values.reshape((2,) * count + values.shape[1:])
    for bit in order[::-1]:
        axis = count - 1 - bit
        mine = own_bit(bit)
        sent = lax.dynamic_index_in_dim(held, 1 - mine, axis).astype(wire)
        kept = lax.dynamic_index_in_dim(held, mine, axis)
        held = kept.astype(jnp.float32) + swap(sent, bit, parts).astype(jnp.float32)
    return held.reshape(held.shape[count:])


def gather_rows(values, parts):
    rows, columns = values.shape
    first = columns * 3 // 8
    pieces = [
        gather_bits(values[:, low:high], order, parts).reshape(parts * rows, high - low)
        for low, high, order in zip(
            (0, first, 2 * first), (first, 2 * first, columns), orders(parts)
        )
    ]
    return jnp.concatenate(pieces, axis=1)


def scatter_rows(values, parts):
    rows, columns = values.shape
    split = values.reshape(parts, rows // parts, columns)
    first = columns * 3 // 8
    pieces = [
        scatter_bits(split[:, :, low:high], order, parts, jnp.bfloat16)
        for low, high, order in zip(
            (0, first, 2 * first), (first, 2 * first, columns), orders(parts)
        )
    ]
    return jnp.concatenate(pieces, axis=1)


def across(values):
    return lax.ppermute(values, "tensor", [(0, 1), (1, 0)])


def join(values, axis=0):
    other = across(values)
    return jnp.where(
        lax.axis_index("tensor") == 0,
        jnp.concatenate((values, other), axis),
        jnp.concatenate((other, values), axis),
    )


def half(values, index):
    rows = values.shape[0] // 2
    return lax.dynamic_slice_in_dim(values, index * rows, rows, 0)


def reduce_halves(product, values):
    here = lax.axis_index("tensor")
    other = across(product(half(values, 1 - here)).astype(jnp.bfloat16))
    return product(half(values, here)) + other.astype(jnp.float32)


def shared_factor(partial, parts):
    count = partial.shape[0]
    extra = -count % parts
    if extra:
        partial = jnp.pad(partial, ((0, extra), (0, 0), (0, 0)))
    split = partial.reshape((parts, -1) + partial.shape[1:])
    order = orders(parts)[0]
    raw = scatter_bits(split, order, parts, jnp.float32)
    factor = gather_bits(gram_factor(raw), order, parts)
    return factor.reshape(partial.shape)[:count]


def adam_step(param, gradient, first, second, count):
    first_new = beta_first * first + (1.0 - beta_first) * gradient
    second_new = beta_second * second + (1.0 - beta_second) * gradient * gradient
    corr_one = 1.0 - jnp.power(beta_first, count)
    corr_two = 1.0 - jnp.power(beta_second, count)
    change = adam_rate * (first_new / corr_one) / (jnp.sqrt(second_new / corr_two) + adam_eps)
    return (param - change, first_new, second_new)


def per_device(
    tokens,
    lengths,
    cotangent,
    query_key_value,
    dense_weight,
    expand_weight,
    shrink_weight,
    query_value_bias,
    expand_bias,
    small_params,
    query_key_value_moment,
    dense_moment,
    expand_moment,
    shrink_moment,
    small_first,
    small_second,
    bias_first,
    bias_second,
    expand_first,
    expand_second,
    step_count,
):
    pieces = lax.axis_size("tensor")
    local_rows = tokens.shape[1]
    seq_rows = local_rows * pieces
    width = tokens.shape[2]
    head_cols = query_key_value.shape[2]
    heads_here = head_cols // HD
    block = min(512, seq_rows)
    length = lengths[0]
    here = lax.axis_index("tensor")
    positions = here * local_rows + jnp.arange(local_rows, dtype=jnp.int32)
    valid = (positions < length).astype(jnp.float32)[:, None]
    head_index = here * heads_here + jnp.arange(heads_here, dtype=jnp.int32) + 1
    slopes = jnp.exp2(-8.0 * head_index.astype(jnp.float32) / H)
    low_triple = query_key_value.astype(jnp.bfloat16)
    low_dense = dense_weight.astype(jnp.bfloat16)
    low_expand = expand_weight.astype(jnp.bfloat16)
    low_shrink = shrink_weight.astype(jnp.bfloat16)
    low_shift = expand_bias.astype(jnp.bfloat16)
    pair_small = join(small_params.astype(jnp.bfloat16), 1)
    extras = jnp.concatenate((low_shift, pair_small.reshape(-1)))
    extra_rows = -(-extras.shape[0] // head_cols)
    extras = jnp.pad(extras, (0, extra_rows * head_cols - extras.shape[0]))
    groups = lax.axis_size("dp")
    order_one, order_two, order_three = orders(groups)
    side = head_cols // 2
    first_part = gather_bits(
        jnp.concatenate((low_triple[:, 0], low_dense[:, :side]), axis=1), order_one, groups
    ).reshape(width, head_cols + side)
    second_part = gather_bits(
        jnp.concatenate((low_triple[:, 1], low_dense[:, side:]), axis=1), order_two, groups
    ).reshape(width, head_cols + side)
    third_part = gather_bits(
        jnp.concatenate((low_triple[:, 2], extras.reshape(extra_rows, head_cols)), axis=0),
        order_three,
        groups,
    )
    part_rows = low_triple.shape[0]
    packed_extras = third_part[:, part_rows:].reshape(groups, extra_rows * head_cols)
    triple = jnp.concatenate(
        (
            first_part[:, :head_cols],
            second_part[:, :head_cols],
            third_part[:, :part_rows].reshape(width, head_cols),
        ),
        axis=1,
    )
    dense = jnp.concatenate((first_part[:, head_cols:], second_part[:, head_cols:]), axis=1)
    shifts = low_shift.shape[0]
    expand_shift = packed_extras[:, :shifts].reshape(-1)
    smalls = pair_small.size
    small = (
        packed_extras[:, shifts : shifts + smalls]
        .reshape((groups,) + pair_small.shape)
        .transpose(1, 0, 2)
        .reshape(pair_small.shape[0], width)
        .astype(jnp.float32)
    )
    shrink = lax.all_gather(low_shrink, "dp", axis=0, tiled=True)
    expand = gather_rows(low_expand, groups)
    query_shift = lax.optimization_barrier(query_value_bias.astype(jnp.bfloat16)).astype(
        jnp.float32
    )
    shift_values = expand_shift.astype(jnp.float32)
    inputs = tokens[0].astype(jnp.float32)
    normed_one, inverse_one = normalize(inputs)
    hidden_one = join((normed_one * small[0] + small[1]).astype(jnp.bfloat16))
    grad_result = valid * cotangent[0].astype(jnp.float32)
    grad_feed = grad_result.astype(jnp.bfloat16)
    grad_feed_all = join(grad_feed)
    projected = jnp.dot(hidden_one, triple, preferred_element_type=jnp.float32)
    split_heads = (seq_rows, heads_here, HD)
    queries = (
        (projected[:, :head_cols] + query_shift[0]).astype(jnp.bfloat16).reshape(split_heads)
    )
    keys = projected[:, head_cols : 2 * head_cols].astype(jnp.bfloat16).reshape(split_heads)
    values = (
        (projected[:, 2 * head_cols :] + query_shift[1]).astype(jnp.bfloat16).reshape(split_heads)
    )
    mixed, logsum = attend(queries, keys, values, length, slopes, block)
    mixed_flat = mixed.reshape(seq_rows, head_cols)
    residual = inputs + (
        reduce_halves(
            lambda part: lax.dot_general(
                part, dense, contract_last, preferred_element_type=jnp.float32
            ),
            mixed_flat,
        )
        + small[2]
    )
    normed_two, inverse_two = normalize(residual)
    hidden_local = (normed_two * small[3] + small[4]).astype(jnp.bfloat16)
    hidden_two = join(hidden_local)
    expanded = (
        lax.dot_general(hidden_two, expand, contract_last, preferred_element_type=jnp.float32)
        + shift_values
    )
    activated = jax.nn.gelu(expanded, approximate=True).astype(jnp.bfloat16)
    feed = reduce_halves(
        lambda part: jnp.dot(part, shrink, preferred_element_type=jnp.float32), activated
    )
    grad_act = lax.dot_general(
        grad_feed_all, shrink, contract_last, preferred_element_type=jnp.float32
    )
    shrink_grad = lax.dot_general(
        activated, grad_feed_all, contract_first, preferred_element_type=jnp.float32
    )
    grad_expanded = (grad_act * gelu_slope(expanded)).astype(jnp.bfloat16)
    expand_grad = lax.dot_general(
        grad_expanded, hidden_two, contract_first, preferred_element_type=jnp.float32
    )
    grad_hidden_two = reduce_halves(
        lambda part: jnp.dot(part, expand, preferred_element_type=jnp.float32), grad_expanded
    )
    shift_grad = jnp.sum(grad_expanded.astype(jnp.float32), axis=0)
    output = (valid * (residual + (feed + small[5]))).astype(jnp.bfloat16)[None]
    grad_residual = grad_result + norm_back(grad_hidden_two, normed_two, inverse_two, small[3])
    grad_branch = grad_residual.astype(jnp.bfloat16)
    grad_branch_all = join(grad_branch)
    dense_grad = lax.dot_general(
        grad_branch_all, mixed_flat, contract_first, preferred_element_type=jnp.float32
    )
    grad_mixed = (
        jnp.dot(grad_branch_all, dense, preferred_element_type=jnp.float32)
        .astype(jnp.bfloat16)
        .reshape(seq_rows, heads_here, HD)
    )
    grad_queries, grad_keys, grad_values = attend_back(
        queries, keys, values, grad_mixed, logsum, length, slopes, block
    )
    grad_parts = tuple(
        part.reshape(seq_rows, head_cols) for part in (grad_queries, grad_keys, grad_values)
    )
    grad_projected = jnp.concatenate(grad_parts, axis=1)
    bias_grad_local = jnp.stack(
        (
            jnp.sum(grad_parts[0].astype(jnp.float32), axis=0),
            jnp.sum(grad_parts[2].astype(jnp.float32), axis=0),
        )
    )
    triple_sum = jnp.stack(
        [
            scatter_bits(
                lax.dot_general(
                    hidden_one, part, contract_first, preferred_element_type=jnp.float32
                ).reshape(groups, part_rows, head_cols),
                order,
                groups,
                jnp.bfloat16,
            )
            for part, order in zip(grad_parts, orders(groups))
        ],
        axis=1,
    )
    grad_hidden_one = reduce_halves(
        lambda part: lax.dot_general(
            part, triple, contract_last, preferred_element_type=jnp.float32
        ),
        grad_projected,
    )
    input_grad = grad_residual + norm_back(grad_hidden_one, normed_one, inverse_one, small[0])
    small_terms = jnp.stack(
        (
            jnp.sum(grad_hidden_one * normed_one, axis=0),
            jnp.sum(grad_hidden_one, axis=0),
            jnp.sum(grad_branch.astype(jnp.float32), axis=0),
            jnp.sum(grad_hidden_two * normed_two, axis=0),
            jnp.sum(grad_hidden_two, axis=0),
            jnp.sum(grad_feed.astype(jnp.float32), axis=0),
        )
    )
    small_cols = small_params.shape[1]
    split_small = small_terms.reshape(6, groups, pieces, small_cols).transpose(2, 1, 0, 3)
    other_small = across(lax.dynamic_index_in_dim(split_small, 1 - here, 0, keepdims=False))
    small_own = lax.dynamic_index_in_dim(split_small, here, 0, keepdims=False) + other_small
    sums = jnp.concatenate(
        (small_own.reshape(-1), shift_grad, bias_grad_local.reshape(-1))
    ).reshape(-1, 128)
    for bit in range(bits_of(groups)):
        sums = sums + swap(sums, bit, groups)
    sums = sums.reshape(-1)
    group = lax.axis_index("dp")
    small_count = groups * 6 * small_cols
    small_grad = lax.dynamic_slice_in_dim(
        sums[:small_count], group * 6 * small_cols, 6 * small_cols
    ).reshape(6, small_cols)
    shift_count = shift_grad.shape[0]
    shift_sum = lax.dynamic_slice_in_dim(
        sums[small_count : small_count + shift_count], group * shifts, shifts
    )
    bias_sum = sums[small_count + shift_count :].reshape(2, head_cols)
    shrink_sum = lax.psum_scatter(
        shrink_grad.astype(jnp.bfloat16), "dp", scatter_dimension=0, tiled=True
    ).astype(jnp.float32)
    expand_sum = scatter_rows(expand_grad, groups)
    dense_sum = scatter_bits(
        dense_grad.reshape(groups, part_rows, head_cols), order_two, groups, jnp.bfloat16
    )
    count = step_count[0].astype(jnp.float32)
    rows_here = triple_sum.shape[0]
    triple_moment = decay_rate * query_key_value_moment + triple_sum
    dense_moment_new = decay_rate * dense_moment + dense_sum
    expand_moment_new = decay_rate * expand_moment + expand_sum
    shrink_moment_new = decay_rate * shrink_moment + shrink_sum
    head_update = jnp.concatenate(
        (
            (triple_sum + decay_rate * triple_moment).reshape(rows_here, 3 * heads_here, HD),
            (dense_sum + decay_rate * dense_moment_new).reshape(rows_here, heads_here, HD),
        ),
        axis=1,
    )
    feed_rows = expand_sum.shape[0]
    feed_blocks = width // HD
    feed_update = jnp.stack(
        (expand_sum + decay_rate * expand_moment_new, shrink_sum + decay_rate * shrink_moment_new)
    )
    feed_update = (
        feed_update.reshape(2, feed_rows, feed_blocks, HD)
        .transpose(1, 0, 2, 3)
        .reshape(feed_rows, 2 * feed_blocks, HD)
    )
    head_factor = shared_factor(block_gram(head_update), groups)
    feed_gram = block_gram(feed_update)
    feed_half = half(feed_gram, here) + across(half(feed_gram, 1 - here))
    feed_factor = join(shared_factor(feed_half, groups))
    head_ortho = jnp.einsum("rbi,bij->rbj", head_update, head_factor, precision=highest)
    feed_ortho = jnp.einsum("rbi,bij->rbj", feed_update, feed_factor, precision=highest)
    head_change = head_ortho * (muon_rate * math.sqrt(max(1.0, width / HD)))
    triple_new = query_key_value - head_change[:, : 3 * heads_here].reshape(rows_here, 3, head_cols)
    dense_new = dense_weight - head_change[:, 3 * heads_here :].reshape(rows_here, head_cols)
    feed_change = feed_ortho * (muon_rate * math.sqrt(max(1.0, FF / HD)))
    feed_change = (
        feed_change.reshape(feed_rows, 2, feed_blocks, HD)
        .transpose(1, 0, 2, 3)
        .reshape(2, feed_rows, width)
    )
    expand_new = expand_weight - feed_change[0]
    shrink_new = shrink_weight - feed_change[1]
    small_new, small_first_new, small_second_new = adam_step(
        small_params, small_grad, small_first, small_second, count
    )
    bias_new, bias_first_new, bias_second_new = adam_step(
        query_value_bias, bias_sum, bias_first, bias_second, count
    )
    shift_new, expand_first_new, expand_second_new = adam_step(
        expand_bias, shift_sum, expand_first, expand_second, count
    )
    return (
        output,
        input_grad[None],
        triple_sum,
        dense_sum,
        expand_sum,
        shrink_sum,
        bias_sum,
        shift_sum,
        small_grad,
        triple_new,
        dense_new,
        expand_new,
        shrink_new,
        bias_new,
        shift_new,
        small_new,
        triple_moment,
        dense_moment_new,
        expand_moment_new,
        shrink_moment_new,
        small_first_new,
        small_second_new,
        bias_first_new,
        bias_second_new,
        expand_first_new,
        expand_second_new,
    )


def solution(mesh):
    in_specs = (
        P("dp", "tensor", None),
        P("dp"),
        P("dp", "tensor", None),
        P("dp", None, "tensor"),
        P("dp", "tensor"),
        P(("dp", "tensor"), None),
        P(("dp", "tensor"), None),
        P(None, "tensor"),
        P(("dp", "tensor")),
        P(None, ("dp", "tensor")),
        P("dp", None, "tensor"),
        P("dp", "tensor"),
        P(("dp", "tensor"), None),
        P(("dp", "tensor"), None),
        P(None, ("dp", "tensor")),
        P(None, ("dp", "tensor")),
        P(None, "tensor"),
        P(None, "tensor"),
        P(("dp", "tensor")),
        P(("dp", "tensor")),
        P(),
    )
    out_specs = (
        P("dp", "tensor", None),
        P("dp", "tensor", None),
        P("dp", None, "tensor"),
        P("dp", "tensor"),
        P(("dp", "tensor"), None),
        P(("dp", "tensor"), None),
        P(None, "tensor"),
        P(("dp", "tensor")),
        P(None, ("dp", "tensor")),
        P("dp", None, "tensor"),
        P("dp", "tensor"),
        P(("dp", "tensor"), None),
        P(("dp", "tensor"), None),
        P(None, "tensor"),
        P(("dp", "tensor")),
        P(None, ("dp", "tensor")),
        P("dp", None, "tensor"),
        P("dp", "tensor"),
        P(("dp", "tensor"), None),
        P(("dp", "tensor"), None),
        P(None, ("dp", "tensor")),
        P(None, ("dp", "tensor")),
        P(None, "tensor"),
        P(None, "tensor"),
        P(("dp", "tensor")),
        P(("dp", "tensor")),
    )
    return jax.shard_map(
        per_device, mesh=mesh, in_specs=in_specs, out_specs=out_specs, check_vma=False
    )
```
